256 devices in a mesh: section: 8 (over z), dp: 32 (over x, y, core).
Axes of the slice: x: 4, y: 4, z: 8, core: 2. Of those that a mesh axis runs over, the one named last changes fastest.
Arguments:
- tokens: bfloat16 [4096, 5120], P('dp'), may hold values from -6 to 6
- cotangent: bfloat16 [4096, 5120], P('dp'), may hold values from -0.75 to 0.75
- section_layers: int32 [8], P('section'), may hold values from 1 to 2, as said below
- up_rows: int32 [16, 112], P('section'), may hold values from 0 to 39, as said below
- down_cols: int32 [16, 112], P('section'), may hold values from 0 to 39, as said below
- up_blocks: bfloat16 [16, 112, 128, 128], P('section', None, 'dp'), may hold values from -0.5 to 0.5
- down_blocks: bfloat16 [16, 112, 128, 128], P('section', None, 'dp'), may hold values from -0.3125 to 0.3125
Outputs:
- section_outputs: bfloat16 [8, 4096, 5120], P('section', 'dp')
- section_input_grads: bfloat16 [8, 4096, 5120], P('section', 'dp')
- up_grads: bfloat16 [16, 112, 128, 128], P('section', None, 'dp')
- down_grads: bfloat16 [16, 112, 128, 128], P('section', None, 'dp')
The draws below stay inside these ranges and needn't reach their ends.
Inputs may be any that keep to these rules, and one draw needn't show every extreme that they name: `section_layers`: each section applies one or two layers; in every draw some section applies two and some section applies one. `up_rows`: in each layer every feature block is read by 2 or 3 hidden blocks. `down_cols`: in each layer every feature block is written by 2 or 3 hidden blocks.
All inputs are finite; a program needn't handle non-finite values.
Results may differ from the reference program's by a relative error of at most 0.029.
Values may be sent and summed in bfloat16 or wider, within the bound.
No kernel may reach another device: no remote copies, remote signals or barrier semaphores. Data moves between devices by JAX's collectives and lax.ppermute only.
A program may use at most 192 MiB of HBM per device.

```python
import jax
import jax.numpy as jnp
from jax import lax

D = 5120
FF = 14336
BLK = 128
TOK_DEV = 128
DB = 40
FB = 112
SECTIONS = 8
LAYERS = 16
TOKENS = 4096
N_DP = 32


def block_pattern(key):
    keys = jax.random.split(key, LAYERS)
    return jax.vmap(lambda one: jax.random.permutation(one, FB) % DB)(keys).astype(jnp.int32)


def draw_up_rows(key, part):
    return block_pattern(jax.random.fold_in(key, 11))


def draw_down_cols(key, part):
    return block_pattern(jax.random.fold_in(key, 12))


def draw_section_layers(key, part):
    keys = jax.random.split(jax.random.fold_in(key, 13), 3)
    base = jax.random.randint(keys[0], (SECTIONS,), 1, 3)
    high_section = jax.random.randint(keys[1], (), 0, SECTIONS)
    low_section = (high_section + 1 + jax.random.randint(keys[2], (), 0, SECTIONS - 1)) % SECTIONS
    base = base.at[high_section].set(2)
    base = base.at[low_section].set(1)
    return base.astype(jnp.int32)


def block_levels(rng, dims, cuts, smallest, high):
    factor_of, own = 1.0, jax.random.fold_in(rng, 6)
    for dim, parts in cuts:
        steps = jnp.exp(jax.random.uniform(jax.random.fold_in(own, dim), (parts,), jnp.float32, smallest / len(cuts), high / len(cuts)))
        factor_of = factor_of * jnp.repeat(steps, dims[dim] // parts).reshape([-1 if axis == dim else 1 for axis in range(len(dims))])
    return factor_of


def noise(own_key, shape, width, bound, shards=(), kind=jnp.bfloat16):
    loudness = block_levels(own_key, shape, shards, -0.22, 0.18) if shards else 1.0
    array = jax.random.normal(own_key, shape, jnp.float32) * width * loudness
    return jnp.minimum(jnp.maximum(array, -bound), bound).astype(kind)


def setup_inputs(seed: int = 0) -> dict:
    seeds = jax.random.split(jax.random.key(seed), 8)
    tokens = noise(seeds[0], (TOKENS, D), 1.0, 6.0, ((0, 32),))
    cotangent = noise(seeds[1], (TOKENS, D), 0.125, 0.75, ((0, 32),))
    section_layers = draw_section_layers(jax.random.fold_in(seeds[7], 71), 0)
    up_rows = draw_up_rows(jax.random.fold_in(seeds[7], 71), 0)
    down_cols = draw_down_cols(jax.random.fold_in(seeds[7], 71), 0)
    up_blocks = noise(seeds[5], (LAYERS, FB, BLK, BLK), BLK ** -0.5, 0.5, ((0, 8), (2, 32)))
    down_blocks = noise(seeds[6], (LAYERS, FB, BLK, BLK), (BLK * FB // DB) ** -0.5, 0.3125, ((0, 8), (2, 32)))
    return {"tokens": tokens, "cotangent": cotangent, "section_layers": section_layers, "up_rows": up_rows, "down_cols": down_cols, "up_blocks": up_blocks, "down_blocks": down_blocks}


root_coef = 0.7978845608028654
cubic_coef = 0.044715

def gelu_parts(inputs):
    inner = root_coef * (inputs + cubic_coef * inputs * inputs * inputs)
    tangent = jnp.tanh(inner)
    values = 0.5 * inputs * (1.0 + tangent)
    slope = 0.5 * (1.0 + tangent) + 0.5 * inputs * (1.0 - tangent * tangent) * root_coef * (1.0 + 3.0 * cubic_coef * inputs * inputs)
    return (values, slope)

def one_hot(indices, count):
    return (indices[:, None] == jnp.arange(count, dtype=jnp.int32)[None, :]).astype(jnp.float32)

def layer_parts(hidden, w_up, row_ids):
    count_rows = hidden.shape[0]
    hidden_f = hidden.astype(jnp.float32)
    inv_rms = lax.rsqrt(lax.optimization_barrier(jnp.mean(hidden_f * hidden_f, axis=-1, keepdims=True)) + 1e-05)
    normal = hidden_f * inv_rms
    normed = normal.astype(jnp.bfloat16)
    picked = jnp.take(normed.reshape(count_rows, D // BLK, BLK), row_ids, axis=1)
    pre_act = jnp.einsum('rfi,fio->rfo', picked.astype(jnp.float32), w_up.astype(jnp.float32))
    return (hidden_f, inv_rms, normal, picked, pre_act)

def layer_forward(hidden, w_up, w_down, row_ids, col_ids):
    count_rows = hidden.shape[0]
    hidden_f, inv_rms, normal, picked, pre_act = layer_parts(hidden, w_up, row_ids)
    values, slope = gelu_parts(pre_act)
    gated = values.astype(jnp.bfloat16)
    mixed = jnp.einsum('rfi,fio->rfo', gated.astype(jnp.float32), w_down.astype(jnp.float32))
    summed = jnp.einsum('rfo,fd->rdo', mixed, one_hot(col_ids, D // BLK), precision=lax.Precision.HIGHEST)
    return (hidden_f + summed.reshape(count_rows, D)).astype(jnp.bfloat16)

def layer_backward(hidden, cot, w_up, w_down, row_ids, col_ids):
    count_rows = hidden.shape[0]
    hidden_f, inv_rms, normal, picked, pre_act = layer_parts(hidden, w_up, row_ids)
    values, slope = gelu_parts(pre_act)
    gated = values.astype(jnp.bfloat16)
    cot_picked = jnp.take(cot.reshape(count_rows, D // BLK, BLK), col_ids, axis=1)
    d_gated = jnp.einsum('rfo,fio->rfi', cot_picked.astype(jnp.float32), w_down.astype(jnp.float32))
    grad_down = jnp.einsum('rfi,rfo->fio', gated.astype(jnp.float32), cot_picked.astype(jnp.float32))
    d_pre = (d_gated * slope).astype(jnp.bfloat16)
    grad_up = jnp.einsum('rfi,rfo->fio', picked.astype(jnp.float32), d_pre.astype(jnp.float32))
    d_picked = jnp.einsum('rfo,fio->rfi', d_pre.astype(jnp.float32), w_up.astype(jnp.float32))
    d_normal = jnp.einsum('rfi,fd->rdi', d_picked, one_hot(row_ids, D // BLK), precision=lax.Precision.HIGHEST).reshape(count_rows, D)
    d_hidden = cot.astype(jnp.float32) + inv_rms * (d_normal - normal * lax.optimization_barrier(jnp.mean(d_normal * normal, axis=-1, keepdims=True)))
    return (d_hidden.astype(jnp.bfloat16), grad_up, grad_down)

def reference(tokens, cotangent, section_layers, up_rows, down_cols, up_blocks, down_blocks):

    def params(layer):
        return (up_blocks[layer], down_blocks[layer], up_rows[layer], down_cols[layer])

    def run_block(totals, block_idx):
        start = (block_idx * TOK_DEV).astype(jnp.int32)
        current = lax.dynamic_slice_in_dim(tokens, start, TOK_DEV, 0)
        cot = lax.dynamic_slice_in_dim(cotangent, start, TOK_DEV, 0)
        section_in = []
        section_out = []
        for section_num in range(SECTIONS):
            first = 2 * section_num
            section_in.append(current)
            w_up, w_down, row_ids, col_ids = params(first)
            after_one = layer_forward(current, w_up, w_down, row_ids, col_ids)
            w_up, w_down, row_ids, col_ids = params(first + 1)
            after_two = layer_forward(after_one, w_up, w_down, row_ids, col_ids)
            current = jnp.where(section_layers[section_num] > 1, after_two, after_one)
            section_out.append(current)
        grads_up = [None] * LAYERS
        grads_down = [None] * LAYERS
        in_grads = [None] * SECTIONS
        for section_num in reversed(range(SECTIONS)):
            first = 2 * section_num
            active = section_layers[section_num] > 1
            w_up, w_down, row_ids, col_ids = params(first)
            after_one = layer_forward(section_in[section_num], w_up, w_down, row_ids, col_ids)
            w_up2, w_down2, row_ids2, col_ids2 = params(first + 1)
            cot_two, up_two, down_two = layer_backward(after_one, cot, w_up2, w_down2, row_ids2, col_ids2)
            cot_mid = jnp.where(active, cot_two, cot)
            grads_up[first + 1] = jnp.where(active, up_two, 0.0)
            grads_down[first + 1] = jnp.where(active, down_two, 0.0)
            cot, up_one, down_one = layer_backward(section_in[section_num], cot_mid, w_up, w_down, row_ids, col_ids)
            grads_up[first] = up_one
            grads_down[first] = down_one
            in_grads[section_num] = cot
        partial_up = lax.optimization_barrier(jnp.stack(grads_up).astype(jnp.bfloat16)).astype(jnp.float32)
        partial_down = lax.optimization_barrier(jnp.stack(grads_down).astype(jnp.bfloat16)).astype(jnp.float32)
        return ((totals[0] + partial_up, totals[1] + partial_down), (jnp.stack(section_out), jnp.stack(in_grads)))
    zeros = jnp.zeros((LAYERS, FF // BLK, BLK, BLK), jnp.float32)
    totals, stacked = lax.scan(run_block, (zeros, zeros), jnp.arange(N_DP, dtype=jnp.int32))
    outs = jnp.transpose(stacked[0], (1, 0, 2, 3)).reshape(SECTIONS, TOKENS, D)
    grads_in = jnp.transpose(stacked[1], (1, 0, 2, 3)).reshape(SECTIONS, TOKENS, D)
    return (outs, grads_in, totals[0].astype(jnp.bfloat16), totals[1].astype(jnp.bfloat16))
```

```python
import functools

import jax
import jax.numpy as jnp
from jax import lax
from jax.experimental import pallas as pl
from jax.experimental.pallas import tpu as pltpu
from jax.sharding import PartitionSpec as P

GROUPS = 4
UNROLL = 28
EPS = 1e-05
SIDE = 4

root_coef = 0.7978845608028654
cubic_coef = 0.044715

HBM = pl.BlockSpec(memory_space=pltpu.HBM)
SMEM = pl.BlockSpec(memory_space=pltpu.SMEM)
NN = (((1,), (0,)), ((), ()))
NT = (((1,), (1,)), ((), ()))
TN = (((0,), (0,)), ((), ()))


def dot(a, b, dims):
    return lax.dot_general(a, b, dims, preferred_element_type=jnp.float32)


def gelu_parts(p):
    square = p * p
    tangent = jnp.tanh(p * (root_coef + (root_coef * cubic_coef) * square))
    half = 0.5 * p
    gate = 0.5 + 0.5 * tangent
    slope = gate + half * (1.0 - tangent * tangent) * (
        root_coef + (3.0 * root_coef * cubic_coef) * square
    )
    return p * gate, slope


def lanes(block):
    return pl.ds(pl.multiple_of(block * 128, 128), 128)


def each_block(count, body, init, step=10):
    def run(i, carry):
        for u in range(step):
            carry = body(i * step + u, carry)
        return carry

    return lax.fori_loop(0, count // step, run, init)


def inverse_rms(h):
    rows, width = h.shape

    def add(k, totals):
        value = h[:, lanes(k)].astype(jnp.float32)
        return totals[1], totals[0] + value * value

    zero = jnp.zeros((rows, 128), jnp.float32)
    one, two = each_block(width // 128, add, (zero, zero))
    return lax.rsqrt(jnp.sum(one + two, axis=1, keepdims=True) * (1.0 / width) + EPS)


def weight_copy(weights, held, sems, l, which, j):
    count = weights.shape[0] // 4
    part = pl.ds((2 * l + which) * count + j * UNROLL, UNROLL)
    return pltpu.make_async_copy(weights.at[part], held.at[part], sems.at[l, which, j])


def load_weights(weights, held, sems, l):
    for j in range(weights.shape[0] // 4 // UNROLL):
        for which in range(2):
            weight_copy(weights, held, sems, l, which, j).start()


def run_pairs(count, before, body):
    def group(j, _):
        before(j)
        for u in range(0, UNROLL, 2):
            body(j * UNROLL + u)
        return 0

    lax.fori_loop(0, count // UNROLL, group, 0)


def pair_dot(left, right, weights, dims):
    rows = left.shape[0]
    both = jnp.concatenate([left, right], axis=0)
    axis = 1 if dims is NN else 0
    wide = dot(both, jnp.concatenate(weights, axis=axis), dims)
    return wide[:rows, :128], wide[rows:, 128:]


def forward_kernel(tick, meta, ups, downs, tok, inc, weights, after, *refs):
    (_, _, _, _, _, y, kin, kmid, kout, slope, gated,
     xv, held, normed, acc, sv, gv, wsem, ssem, gsem, iosem) = refs
    section = meta[0]
    mb = tick - section
    live = (mb >= 0) & (mb < GROUPS)
    layers = meta[1]
    two = layers > 1
    count, width = ups.shape[1], xv.shape[2]

    def io(n, src, dst):
        return pltpu.make_async_copy(src, dst, iosem.at[n])

    def save_slope(l):
        return pltpu.make_async_copy(sv.at[l], slope.at[l, :, mb], ssem.at[l])

    def save_gated(l):
        return pltpu.make_async_copy(gv.at[l], gated.at[l, :, mb], gsem.at[l])

    def layer(l, _):
        x, out = xv.at[l], xv.at[l + 1]
        inv = inverse_rms(x)

        def start(k, _):
            value = x[:, lanes(k)].astype(jnp.float32)
            normed[:, lanes(k)] = (value * inv).astype(jnp.bfloat16)
            acc[:, lanes(k)] = value
            return 0

        each_block(width // 128, start, 0)
        up_at, down_at = 2 * l * count, (2 * l + 1) * count

        def body(f):
            pres = pair_dot(
                normed[:, lanes(ups[l, f])],
                normed[:, lanes(ups[l, f + 1])],
                (held[up_at + f], held[up_at + f + 1]),
                NN,
            )
            values = []
            for q, pre in enumerate(pres):
                value, grad = gelu_parts(pre)
                values.append(value.astype(jnp.bfloat16))
                gv[l, f + q] = values[q]
                sv[l, f + q] = grad.astype(jnp.bfloat16)
            mixed = pair_dot(
                *values, (held[down_at + f], held[down_at + f + 1]), NN
            )
            for q in range(2):
                at = lanes(downs[l, f + q])
                acc[:, at] = acc[:, at] + mixed[q]

        def before(j):
            for which in range(2):
                weight_copy(weights, held, wsem, l, which, j).wait()

        run_pairs(count, before, body)
        save_slope(l).start()
        save_gated(l).start()

        def finish(k, _):
            out[:, lanes(k)] = acc[:, lanes(k)].astype(jnp.bfloat16)
            return 0

        each_block(width // 128, finish, 0)
        return 0

    @pl.when(live)
    def _():
        @pl.when(section == 0)
        def _():
            io(0, tok.at[mb], xv.at[0]).start()

        @pl.when(section != 0)
        def _():
            io(0, inc, xv.at[0]).start()

        load_weights(weights, held, wsem, 0)

        @pl.when(two)
        def _():
            load_weights(weights, held, wsem, 1)

        io(0, inc, xv.at[0]).wait()
        io(1, xv.at[0], kin.at[mb]).start()
        lax.fori_loop(0, layers, layer, 0)
        io(2, xv.at[layers], y).start()
        io(3, xv.at[layers], kout.at[mb]).start()

        @pl.when(two)
        def _():
            io(4, xv.at[1], kmid.at[mb]).start()
            io(4, xv.at[1], kmid.at[mb]).wait()
            save_slope(1).wait()
            save_gated(1).wait()

        io(2, xv.at[layers], y).wait()
        io(3, xv.at[layers], kout.at[mb]).wait()
        io(1, xv.at[0], kin.at[mb]).wait()
        save_slope(0).wait()
        save_gated(0).wait()


def backward_kernel(tick, last, meta, ups, downs, cotg, inc, weights, kin, kmid, slope, *refs):
    (_, _, _, _, dx, kdx, ktop, kinner, dpre,
     cv, hv, held, acc, sv, dv, wsem, ssem, dsem, iosem) = refs
    section = meta[0]
    mb = tick - (last - section)
    live = (mb >= 0) & (mb < GROUPS)
    layers = meta[1]
    two = layers > 1
    count, width = ups.shape[1], cv.shape[2]
    rows = cv.shape[1]

    def io(n, src, dst):
        return pltpu.make_async_copy(src, dst, iosem.at[n])

    def load_slope(l):
        return pltpu.make_async_copy(slope.at[l, :, mb], sv.at[l], ssem.at[l])

    def save_dpre(l):
        return pltpu.make_async_copy(dv.at[l], dpre.at[l, :, mb], dsem.at[l])

    def load_hidden(l, kept):
        return io(1 + l, kept.at[mb], hv.at[l])

    def layer(i, _):
        l = layers - 1 - i
        h, cot, out = hv.at[l], cv.at[l + 1], cv.at[l]
        load_hidden(l, kin).wait()
        inv = inverse_rms(h)

        def blank(k, _):
            acc[:, lanes(k)] = jnp.zeros((rows, 128), jnp.float32)
            return 0

        each_block(width // 128, blank, 0)
        load_slope(l).wait()
        up_at, down_at = 2 * l * count, (2 * l + 1) * count

        def body(f):
            inners = pair_dot(
                cot[:, lanes(downs[l, f])],
                cot[:, lanes(downs[l, f + 1])],
                (held[down_at + f], held[down_at + f + 1]),
                NT,
            )
            values = []
            for q, inner in enumerate(inners):
                scaled = inner * sv[l, f + q].astype(jnp.float32)
                values.append(scaled.astype(jnp.bfloat16))
                dv[l, f + q] = values[q]
            mixed = pair_dot(*values, (held[up_at + f], held[up_at + f + 1]), NT)
            for q in range(2):
                at = lanes(ups[l, f + q])
                acc[:, at] = acc[:, at] + mixed[q]

        def before(j):
            for which in range(2):
                weight_copy(weights, held, wsem, l, which, j).wait()

        run_pairs(count, before, body)
        save_dpre(l).start()

        def dots(k, totals):
            value = acc[:, lanes(k)] * h[:, lanes(k)].astype(jnp.float32)
            return totals[1], totals[0] + value

        zero = jnp.zeros((rows, 128), jnp.float32)
        one, other = each_block(width // 128, dots, (zero, zero))
        mean = jnp.sum(one + other, axis=1, keepdims=True) * inv * (1.0 / width)

        def finish(k, _):
            normal = h[:, lanes(k)].astype(jnp.float32) * inv
            value = cot[:, lanes(k)].astype(jnp.float32) + inv * (
                acc[:, lanes(k)] - normal * mean
            )
            out[:, lanes(k)] = value.astype(jnp.bfloat16)
            return 0

        each_block(width // 128, finish, 0)
        return 0

    @pl.when(live)
    def _():
        @pl.when(section == last)
        def _():
            io(0, cotg.at[mb], cv.at[layers]).start()

        @pl.when(section != last)
        def _():
            io(0, inc, cv.at[layers]).start()

        @pl.when(two)
        def _():
            load_hidden(1, kmid).start()
            load_slope(1).start()
            load_weights(weights, held, wsem, 1)

        load_hidden(0, kin).start()
        load_slope(0).start()
        load_weights(weights, held, wsem, 0)
        io(0, inc, cv.at[layers]).wait()
        lax.fori_loop(0, layers, layer, 0)
        io(5, cv.at[0], dx).start()
        io(6, cv.at[0], kdx.at[mb]).start()
        io(4, cv.at[1], kinner.at[mb]).start()

        @pl.when(two)
        def _():
            io(3, cv.at[2], ktop.at[mb]).start()
            io(3, cv.at[2], ktop.at[mb]).wait()
            save_dpre(1).wait()

        io(5, cv.at[0], dx).wait()
        io(6, cv.at[0], kdx.at[mb]).wait()
        io(4, cv.at[1], kinner.at[mb]).wait()
        save_dpre(0).wait()


def grad_kernel(l, meta, ups, downs, h, cot, gated, dpre, keep, send, normed):
    step = pl.program_id(0)
    count = keep.shape[2]
    width = h.shape[1]
    active = meta[1] > l

    @pl.when(active)
    def _():
        @pl.when(step == 0)
        def _():
            inv = inverse_rms(h)

            def start(k, _):
                normed[:, lanes(k)] = (h[:, lanes(k)].astype(jnp.float32) * inv).astype(
                    jnp.bfloat16
                )
                return 0

            each_block(width // 128, start, 0, 2)

        is_zero = meta[4] == 0
        for u in range(count):
            f = step * count + u
            up = dot(normed[:, lanes(ups[l, f])], dpre[0, u], TN)
            down = dot(gated[0, u], cot[:, lanes(downs[l, f])], TN)
            mine = jnp.where(is_zero, up, down).astype(jnp.bfloat16)
            other = jnp.where(is_zero, down, up).astype(jnp.bfloat16)
            for i in range(SIDE):
                for j in range(SIDE):
                    rows = slice((i * SIDE + j) * 8, (i * SIDE + j) * 8 + 8)
                    keep[i ^ meta[2], j ^ meta[3], u] = mine[rows]
                    send[i ^ meta[2], j ^ meta[3], u] = other[rows]

    @pl.when(jnp.logical_not(active))
    def _():
        keep[...] = jnp.zeros_like(keep)
        send[...] = jnp.zeros_like(send)


def block_grads(l, meta, ups, downs, h, cot, gated, dpre):
    count, width = ups.shape[1], h.shape[1]
    rows, per = h.shape[0], 14
    whole = pl.BlockSpec((rows, width), lambda i: (0, 0))
    table = pl.BlockSpec((1, per, rows, 128), lambda i: (l, i, 0, 0))
    out = pl.BlockSpec((SIDE, SIDE, per, 8, 128), lambda i: (0, 0, i, 0, 0))
    shape = jax.ShapeDtypeStruct((SIDE, SIDE, count, 8, 128), jnp.bfloat16)
    return pl.pallas_call(
        functools.partial(grad_kernel, l),
        grid=(count // per,),
        in_specs=[SMEM, SMEM, SMEM, whole, whole, table, table],
        out_specs=[out, out],
        out_shape=[shape, shape],
        scratch_shapes=[pltpu.VMEM((rows, width), jnp.bfloat16)],
        compiler_params=pltpu.CompilerParams(vmem_limit_bytes=56 << 20),
        name="grads",
    )(meta, ups, downs, h, cot, gated, dpre)


def swap(value, change):
    pairs = []
    for x in range(SIDE):
        for y in range(SIDE):
            for c in range(2):
                a, b, d = change(x, y, c)
                pairs.append(((x * SIDE + y) * 2 + c, (a * SIDE + b) * 2 + d))
    return lax.ppermute(value, "dp", pairs)


def along(axis, bits):
    if axis == 0:
        return lambda x, y, c: (x ^ bits, y, c)
    return lambda x, y, c: (x, y ^ bits, c)


def add(a, b):
    return (a.astype(jnp.float32) + b.astype(jnp.float32)).astype(jnp.bfloat16)


def other_core(value):
    return swap(value, lambda x, y, c: (x, y, 1 - c))


def parts(value, axis, picks):
    return jnp.concatenate(
        [lax.slice_in_dim(value, p, p + 1, axis=axis) for p in picks], axis=axis
    )


def scatter_sum(first, second):
    half = first.shape[2] // 2
    colors = [
        (first[:, :, :half], (1, 0), 1),
        (first[:, :, half:], (1, 0), 3),
        (second[:, :, :half], (0, 1), 1),
        (second[:, :, half:], (0, 1), 3),
    ]
    values = [c[0] for c in colors]
    for stage in range(4):
        fresh = []
        for value, (_, axes, bits) in zip(values, colors):
            axis = axes[stage // 2]
            if stage % 2 == 0:
                send = parts(value, axis, (bits, 2))
                keep = parts(value, axis, (0, bits ^ 2))
                got = swap(send, along(axis, bits))
            else:
                send = parts(value, axis, (1,))
                keep = parts(value, axis, (0,))
                got = swap(send, along(axis, bits ^ 2))
            fresh.append(add(keep, got))
        values = fresh
    shape = (2 * half,) + first.shape[3:]
    return (
        jnp.concatenate(values[:2], axis=2).reshape(shape),
        jnp.concatenate(values[2:], axis=2).reshape(shape),
    )


def blank_arrays(*shapes):
    def kernel(*refs):
        pass

    return pl.pallas_call(
        kernel,
        out_shape=[jax.ShapeDtypeStruct(s, jnp.bfloat16) for s in shapes],
        out_specs=[HBM] * len(shapes),
        name="blank",
    )()


def relay(value, live, steps):
    return lax.ppermute(value, "section", [(s, s + steps) for s in live])


def local(sections, tokens, cotangent, section_layers, up_rows, down_cols, up_blocks, down_blocks):
    last = sections - 1
    tok_rows, width = tokens.shape
    count = up_rows.shape[1]
    groups, rows = GROUPS, tok_rows // GROUPS
    place = lax.axis_index("dp").astype(jnp.int32)
    core = place % 2
    meta = jnp.stack(
        [
            lax.axis_index("section").astype(jnp.int32),
            section_layers[0],
            place // (2 * SIDE),
            (place // 2) % SIDE,
            core,
        ]
    )
    shares = jnp.stack([up_blocks, down_blocks], axis=1).reshape(
        (4 * count,) + up_blocks.shape[2:]
    )
    weights = lax.all_gather(shares, "dp", axis=0)
    weights = jnp.swapaxes(weights, 0, 1).reshape(4 * count, 128, 128)
    tok = tokens.reshape(groups, rows, width)
    cotg = cotangent.reshape(groups, rows, width)
    act = (groups, rows, width)
    table = (2, count, groups, rows, 128)
    bf16 = jnp.bfloat16
    one = jax.ShapeDtypeStruct((rows, width), bf16)
    act_s, table_s = jax.ShapeDtypeStruct(act, bf16), jax.ShapeDtypeStruct(table, bf16)
    dma = pltpu.SemaphoreType.DMA
    params = pltpu.CompilerParams(vmem_limit_bytes=56 << 20)
    flops = 8 * rows * count * 128 * 128
    cost = pl.CostEstimate(flops=flops, bytes_accessed=16 << 20, transcendentals=0)

    def forward(tick, incoming, after, state):
        return pl.pallas_call(
            functools.partial(forward_kernel, tick),
            in_specs=[SMEM] * 3 + [HBM] * 9,
            out_specs=[HBM] * 6,
            out_shape=[one, act_s, act_s, act_s, table_s, table_s],
            scratch_shapes=[
                pltpu.VMEM((3, rows, width), bf16),
                pltpu.VMEM((4 * count, 128, 128), bf16),
                pltpu.VMEM((rows, width), bf16),
                pltpu.VMEM((rows, width), jnp.float32),
                pltpu.VMEM((2, count, rows, 128), bf16),
                pltpu.VMEM((2, count, rows, 128), bf16),
                dma((2, 2, count // UNROLL)),
                dma((2,)),
                dma((2,)),
                dma((5,)),
            ],
            input_output_aliases={7 + i: 1 + i for i in range(5)},
            compiler_params=params,
            cost_estimate=cost,
            name="forward",
        )(meta, up_rows, down_cols, tok, incoming, weights, after, *state)

    def backward(tick, incoming, saved, state):
        return pl.pallas_call(
            functools.partial(backward_kernel, tick, last),
            in_specs=[SMEM] * 3 + [HBM] * 10,
            out_specs=[HBM] * 5,
            out_shape=[one, act_s, act_s, act_s, table_s],
            scratch_shapes=[
                pltpu.VMEM((3, rows, width), bf16),
                pltpu.VMEM((2, rows, width), bf16),
                pltpu.VMEM((4 * count, 128, 128), bf16),
                pltpu.VMEM((rows, width), jnp.float32),
                pltpu.VMEM((2, count, rows, 128), bf16),
                pltpu.VMEM((2, count, rows, 128), bf16),
                dma((2, 2, count // UNROLL)),
                dma((2,)),
                dma((2,)),
                dma((7,)),
            ],
            input_output_aliases={9 + i: 1 + i for i in range(4)},
            compiler_params=params,
            cost_estimate=cost,
            name="backward",
        )(meta, up_rows, down_cols, cotg, incoming, weights, *saved, *state)

    empty, *state = blank_arrays((rows, width), act, act, act, table, table)
    incoming, after = empty, empty
    grad_empty, *grad_state = blank_arrays((rows, width), act, act, act, table)
    grad_incoming = grad_empty
    for tick in range(groups + 2 * last):
        if tick < groups + last:
            result, *state = forward(tick, incoming, after, state)
            live = [s for s in range(last) if 0 <= tick - s < groups]
            if live:
                incoming = relay(result, live, 1)
        back = tick - last
        if back >= 0:
            kin, kmid, _, slope, _ = state
            result, *grad_state = backward(back, grad_incoming, (kin, kmid, slope), grad_state)
            after = result
            live = [s for s in range(1, sections) if 0 <= back - (last - s) < groups]
            if live:
                grad_incoming = relay(result, live, -1)
    kin, kmid, kout, slope, gated = state
    kdx, ktop, kinner, dpre = grad_state

    def flat(a):
        return a.reshape(tok_rows, width)

    gated = gated.reshape(2, count, tok_rows, 128)
    dpre = dpre.reshape(2, count, tok_rows, 128)
    totals = []
    for l, h, cot in ((1, kmid, ktop), (0, kin, kinner)):
        keep, send = block_grads(l, meta, up_rows, down_cols, flat(h), flat(cot), gated, dpre)
        totals.append(add(keep, other_core(send)))
    late, early = scatter_sum(*totals)
    summed = jnp.stack([early, late])
    low, high = summed[:, :, :4], summed[:, :, 4:]
    mine = jnp.where(core == 0, low, high)
    theirs = other_core(jnp.where(core == 0, high, low))
    return (
        kout.reshape(1, tok_rows, width),
        kdx.reshape(1, tok_rows, width),
        jnp.where(core == 0, mine, theirs),
        jnp.where(core == 0, theirs, mine),
    )


def solution(mesh):
    in_specs = (
        P("dp", None),
        P("dp", None),
        P("section"),
        P("section", None),
        P("section", None),
        P("section", None, "dp", None),
        P("section", None, "dp", None),
    )
    out_specs = (
        P("section", "dp", None),
        P("section", "dp", None),
        P("section", None, "dp", None),
        P("section", None, "dp", None),
    )
    step = functools.partial(local, mesh.shape["section"])
    return jax.shard_map(step, mesh=mesh, in_specs=in_specs, out_specs=out_specs, check_vma=False)
```

```python
import functools

import jax
import jax.numpy as jnp
from jax import lax
from jax.experimental import pallas as pl
from jax.experimental.pallas import tpu as pltpu
from jax.sharding import PartitionSpec as P

GROUPS = 4
UNROLL = 28
EPS = 1e-05
SIDE = 4

root_coef = 0.7978845608028654
cubic_coef = 0.044715

HBM = pl.BlockSpec(memory_space=pltpu.HBM)
SMEM = pl.BlockSpec(memory_space=pltpu.SMEM)
VMEM = pl.BlockSpec(memory_space=pltpu.VMEM)
NN = (((1,), (0,)), ((), ()))
NT = (((1,), (1,)), ((), ()))
TN = (((0,), (0,)), ((), ()))


def dot(a, b, dims):
    return lax.dot_general(a, b, dims, preferred_element_type=jnp.float32)


def gelu_parts(p):
    square = p * p
    tangent = jnp.tanh(p * (root_coef + (root_coef * cubic_coef) * square))
    half = 0.5 * p
    gate = 0.5 + 0.5 * tangent
    slope = gate + half * (1.0 - tangent * tangent) * (
        root_coef + (3.0 * root_coef * cubic_coef) * square
    )
    return p * gate, slope


def lanes(block):
    return pl.ds(pl.multiple_of(block * 128, 128), 128)


def each_block(count, body, init, step=10):
    def run(i, carry):
        for u in range(step):
            carry = body(i * step + u, carry)
        return carry

    return lax.fori_loop(0, count // step, run, init)


def inverse_rms(h):
    rows, width = h.shape

    def add(k, totals):
        value = h[:, lanes(k)].astype(jnp.float32)
        return totals[1], totals[0] + value * value

    zero = jnp.zeros((rows, 128), jnp.float32)
    one, two = each_block(width // 128, add, (zero, zero))
    return lax.rsqrt(jnp.sum(one + two, axis=1, keepdims=True) * (1.0 / width) + EPS)


def table_copies(held, table, mb, sems):
    def copy(l, j, out=True):
        part = pl.ds(j * UNROLL, UNROLL)
        here, there = held.at[l, part], table.at[l, part, mb]
        if out:
            return pltpu.make_async_copy(here, there, sems.at[l, j])
        return pltpu.make_async_copy(there, here, sems.at[l, j])

    return copy


def run_pairs(count, before, body, after):
    def group(j, _):
        before(j)
        for u in range(0, UNROLL, 2):
            body(j * UNROLL + u)
        after(j)
        return 0

    lax.fori_loop(0, count // UNROLL, group, 0)


def pair_dot(left, right, weights, dims):
    rows = left.shape[0]
    both = jnp.concatenate([left, right], axis=0)
    axis = 1 if dims is NN else 0
    wide = dot(both, jnp.concatenate(weights, axis=axis), dims)
    return wide[:rows, :128], wide[rows:, 128:]


def forward_kernel(tick, meta, ups, downs, tok, inc, weights, after, *refs):
    (_, _, _, _, _, y, kin, kmid, kout, slope, gated,
     xv, normed, acc, sv, gv, ssem, gsem, iosem) = refs
    section = meta[0]
    mb = tick - section
    live = (mb >= 0) & (mb < GROUPS)
    layers = meta[1]
    two = layers > 1
    count, width = ups.shape[1], xv.shape[2]

    def io(n, src, dst):
        return pltpu.make_async_copy(src, dst, iosem.at[n])

    save_slope = table_copies(sv, slope, mb, ssem)
    save_gated = table_copies(gv, gated, mb, gsem)

    def saved(l):
        for j in range(count // UNROLL):
            save_slope(l, j).wait()
            save_gated(l, j).wait()

    def layer(l, _):
        x, out = xv.at[l], xv.at[l + 1]
        inv = inverse_rms(x)

        def start(k, _):
            value = x[:, lanes(k)].astype(jnp.float32)
            normed[:, lanes(k)] = (value * inv).astype(jnp.bfloat16)
            acc[:, lanes(k)] = value
            return 0

        each_block(width // 128, start, 0)
        up_at, down_at = 2 * l * count, (2 * l + 1) * count

        def body(f):
            pres = pair_dot(
                normed[:, lanes(ups[l, f])],
                normed[:, lanes(ups[l, f + 1])],
                (weights[up_at + f], weights[up_at + f + 1]),
                NN,
            )
            values = []
            for q, pre in enumerate(pres):
                value, grad = gelu_parts(pre)
                values.append(value.astype(jnp.bfloat16))
                gv[l, f + q] = values[q]
                sv[l, f + q] = grad.astype(jnp.bfloat16)
            mixed = pair_dot(
                *values, (weights[down_at + f], weights[down_at + f + 1]), NN
            )
            for q in range(2):
                at = lanes(downs[l, f + q])
                acc[:, at] = acc[:, at] + mixed[q]

        def after(j):
            save_slope(l, j).start()
            save_gated(l, j).start()

        run_pairs(count, lambda j: None, body, after)

        def finish(k, _):
            out[:, lanes(k)] = acc[:, lanes(k)].astype(jnp.bfloat16)
            return 0

        each_block(width // 128, finish, 0)
        return 0

    @pl.when(live)
    def _():
        @pl.when(section == 0)
        def _():
            io(0, tok.at[mb], xv.at[0]).start()

        @pl.when(section != 0)
        def _():
            io(0, inc, xv.at[0]).start()

        io(0, inc, xv.at[0]).wait()
        io(1, xv.at[0], kin.at[mb]).start()
        lax.fori_loop(0, layers, layer, 0)
        io(2, xv.at[layers], y).start()
        io(3, xv.at[layers], kout.at[mb]).start()

        @pl.when(two)
        def _():
            io(4, xv.at[1], kmid.at[mb]).start()
            io(4, xv.at[1], kmid.at[mb]).wait()
            saved(1)

        io(2, xv.at[layers], y).wait()
        io(3, xv.at[layers], kout.at[mb]).wait()
        io(1, xv.at[0], kin.at[mb]).wait()
        saved(0)


def backward_kernel(tick, last, meta, ups, downs, cotg, inc, weights, kin, kmid, slope, *refs):
    (_, _, _, _, dx, kdx, ktop, kinner, dpre,
     cv, hv, acc, sv, dv, ssem, dsem, iosem) = refs
    section = meta[0]
    mb = tick - (last - section)
    live = (mb >= 0) & (mb < GROUPS)
    layers = meta[1]
    two = layers > 1
    count, width = ups.shape[1], cv.shape[2]
    rows = cv.shape[1]

    def io(n, src, dst):
        return pltpu.make_async_copy(src, dst, iosem.at[n])

    slope_copy = table_copies(sv, slope, mb, ssem)
    save_dpre = table_copies(dv, dpre, mb, dsem)

    def load_slope(l):
        for j in range(count // UNROLL):
            slope_copy(l, j, False).start()

    def saved(l):
        for j in range(count // UNROLL):
            save_dpre(l, j).wait()

    def load_hidden(l, kept):
        return io(1 + l, kept.at[mb], hv.at[l])

    def layer(i, _):
        l = layers - 1 - i
        h, cot, out = hv.at[l], cv.at[l + 1], cv.at[l]
        load_hidden(l, kin).wait()
        inv = inverse_rms(h)

        def blank(k, _):
            acc[:, lanes(k)] = jnp.zeros((rows, 128), jnp.float32)
            return 0

        each_block(width // 128, blank, 0)
        up_at, down_at = 2 * l * count, (2 * l + 1) * count

        def body(f):
            inners = pair_dot(
                cot[:, lanes(downs[l, f])],
                cot[:, lanes(downs[l, f + 1])],
                (weights[down_at + f], weights[down_at + f + 1]),
                NT,
            )
            values = []
            for q, inner in enumerate(inners):
                scaled = inner * sv[l, f + q].astype(jnp.float32)
                values.append(scaled.astype(jnp.bfloat16))
                dv[l, f + q] = values[q]
            mixed = pair_dot(*values, (weights[up_at + f], weights[up_at + f + 1]), NT)
            for q in range(2):
                at = lanes(ups[l, f + q])
                acc[:, at] = acc[:, at] + mixed[q]

        run_pairs(
            count,
            lambda j: slope_copy(l, j, False).wait(),
            body,
            lambda j: save_dpre(l, j).start(),
        )

        def dots(k, totals):
            value = acc[:, lanes(k)] * h[:, lanes(k)].astype(jnp.float32)
            return totals[1], totals[0] + value

        zero = jnp.zeros((rows, 128), jnp.float32)
        one, other = each_block(width // 128, dots, (zero, zero))
        mean = jnp.sum(one + other, axis=1, keepdims=True) * inv * (1.0 / width)

        def finish(k, _):
            normal = h[:, lanes(k)].astype(jnp.float32) * inv
            value = cot[:, lanes(k)].astype(jnp.float32) + inv * (
                acc[:, lanes(k)] - normal * mean
            )
            out[:, lanes(k)] = value.astype(jnp.bfloat16)
            return 0

        each_block(width // 128, finish, 0)
        return 0

    @pl.when(live)
    def _():
        @pl.when(section == last)
        def _():
            io(0, cotg.at[mb], cv.at[layers]).start()

        @pl.when(section != last)
        def _():
            io(0, inc, cv.at[layers]).start()

        @pl.when(two)
        def _():
            load_hidden(1, kmid).start()
            load_slope(1)

        load_hidden(0, kin).start()
        load_slope(0)
        io(0, inc, cv.at[layers]).wait()
        lax.fori_loop(0, layers, layer, 0)
        io(5, cv.at[0], dx).start()
        io(6, cv.at[0], kdx.at[mb]).start()
        io(4, cv.at[1], kinner.at[mb]).start()

        @pl.when(two)
        def _():
            io(3, cv.at[2], ktop.at[mb]).start()
            io(3, cv.at[2], ktop.at[mb]).wait()
            saved(1)

        io(5, cv.at[0], dx).wait()
        io(6, cv.at[0], kdx.at[mb]).wait()
        io(4, cv.at[1], kinner.at[mb]).wait()
        saved(0)


def grad_kernel(l, meta, ups, downs, h, cot, gated, dpre, keep, send, normed):
    step = pl.program_id(0)
    count = keep.shape[0]
    width = h.shape[1]
    active = meta[1] > l

    @pl.when(active)
    def _():
        @pl.when(step == 0)
        def _():
            inv = inverse_rms(h)

            def start(k, _):
                normed[:, lanes(k)] = (h[:, lanes(k)].astype(jnp.float32) * inv).astype(
                    jnp.bfloat16
                )
                return 0

            each_block(width // 128, start, 0, 2)

        is_zero = meta[2] == 0
        for u in range(count):
            f = step * count + u
            up = dot(normed[:, lanes(ups[l, f])], dpre[0, u], TN)
            down = dot(gated[0, u], cot[:, lanes(downs[l, f])], TN)
            keep[u] = jnp.where(is_zero, up, down).astype(jnp.bfloat16)
            send[u] = jnp.where(is_zero, down, up).astype(jnp.bfloat16)

    @pl.when(jnp.logical_not(active))
    def _():
        keep[...] = jnp.zeros_like(keep)
        send[...] = jnp.zeros_like(send)


def block_grads(l, meta, ups, downs, h, cot, gated, dpre):
    count, width = ups.shape[1], h.shape[1]
    rows, per = h.shape[0], 14
    whole = pl.BlockSpec((rows, width), lambda i: (0, 0))
    table = pl.BlockSpec((1, per, rows, 128), lambda i: (l, i, 0, 0))
    out = pl.BlockSpec((per, 128, 128), lambda i: (i, 0, 0))
    shape = jax.ShapeDtypeStruct((count, 128, 128), jnp.bfloat16)
    return pl.pallas_call(
        functools.partial(grad_kernel, l),
        grid=(count // per,),
        in_specs=[SMEM, SMEM, SMEM, whole, whole, table, table],
        out_specs=[out, out],
        out_shape=[shape, shape],
        scratch_shapes=[pltpu.VMEM((rows, width), jnp.bfloat16)],
        compiler_params=pltpu.CompilerParams(vmem_limit_bytes=56 << 20),
        name="grads",
    )(meta, ups, downs, h, cot, gated, dpre)


def swap(value, change):
    pairs = []
    for x in range(SIDE):
        for y in range(SIDE):
            for c in range(2):
                a, b, d = change(x, y, c)
                pairs.append(((x * SIDE + y) * 2 + c, (a * SIDE + b) * 2 + d))
    return lax.ppermute(value, "dp", pairs)


def along(axis, bits):
    if axis == 0:
        return lambda x, y, c: (x ^ bits, y, c)
    return lambda x, y, c: (x, y ^ bits, c)


def add(a, b):
    return (a.astype(jnp.float32) + b.astype(jnp.float32)).astype(jnp.bfloat16)


def other_core(value):
    return swap(value, lambda x, y, c: (x, y, 1 - c))


def parts(value, axis, picks):
    return jnp.concatenate(
        [lax.dynamic_slice_in_dim(value, p, 1, axis=axis) for p in picks], axis=axis
    )


def scatter_sum(first, second, place):
    half = first.shape[0] // 2
    colors = [
        (first[:half], (2, 1), 1),
        (first[half:], (2, 1), 3),
        (second[:half], (1, 2), 1),
        (second[half:], (1, 2), 3),
    ]
    values = [c[0] for c in colors]
    for stage in range(4):
        fresh = []
        for value, (_, axes, bits) in zip(values, colors):
            axis = axes[stage // 2]
            me = place[axis - 1]
            if stage % 2 == 0:
                send = parts(value, axis, (me ^ bits, me ^ 2))
                keep = parts(value, axis, (me, me ^ bits ^ 2))
                got = swap(send, along(axis - 1, bits))
            else:
                send = lax.slice_in_dim(value, 1, 2, axis=axis)
                keep = lax.slice_in_dim(value, 0, 1, axis=axis)
                got = swap(send, along(axis - 1, bits ^ 2))
            fresh.append(add(keep, got))
        values = fresh
    shape = (2 * half,) + first.shape[3:]
    return (
        jnp.concatenate(values[:2], axis=0).reshape(shape),
        jnp.concatenate(values[2:], axis=0).reshape(shape),
    )


def blank_arrays(*shapes):
    def kernel(*refs):
        pass

    return pl.pallas_call(
        kernel,
        out_shape=[pltpu.HBM(s, jnp.bfloat16) for s in shapes],
        out_specs=[HBM] * len(shapes),
        compiler_params=pltpu.CompilerParams(vmem_limit_bytes=1 << 20),
        name="blank",
    )()


def far(value):
    return pltpu.with_memory_space_constraint(value, pltpu.HBM)


def relay(value, live, steps):
    moved = lax.ppermute(value, "section", [(s, s + steps) for s in live])
    return pltpu.with_memory_space_constraint(moved, pltpu.VMEM)


def local(sections, tokens, cotangent, section_layers, up_rows, down_cols, up_blocks, down_blocks):
    last = sections - 1
    tok_rows, width = tokens.shape
    count = up_rows.shape[1]
    groups, rows = GROUPS, tok_rows // GROUPS
    place = lax.axis_index("dp").astype(jnp.int32)
    core = place % 2
    meta = jnp.stack(
        [
            lax.axis_index("section").astype(jnp.int32),
            section_layers[0],
            core,
        ]
    )
    shares = jnp.stack([up_blocks, down_blocks], axis=1).reshape(
        (4 * count,) + up_blocks.shape[2:]
    )
    weights = lax.all_gather(shares, "dp", axis=0)
    weights = jnp.swapaxes(weights, 0, 1).reshape(4 * count, 128, 128)
    weights = pltpu.with_memory_space_constraint(weights, pltpu.VMEM)
    tok = tokens.reshape(groups, rows, width)
    cotg = cotangent.reshape(groups, rows, width)
    act = (groups, rows, width)
    table = (2, count, groups, rows, 128)
    bf16 = jnp.bfloat16
    one = pltpu.VMEM((rows, width), bf16)
    act_s, table_s = pltpu.HBM(act, bf16), pltpu.HBM(table, bf16)
    dma = pltpu.SemaphoreType.DMA
    params = pltpu.CompilerParams(vmem_limit_bytes=20 << 20)
    flops = 8 * rows * count * 128 * 128
    cost = pl.CostEstimate(flops=flops, bytes_accessed=16 << 20, transcendentals=0)

    def forward(tick, incoming, after, state):
        return pl.pallas_call(
            functools.partial(forward_kernel, tick),
            in_specs=[SMEM] * 3 + [HBM, VMEM, VMEM] + [HBM] * 6,
            out_specs=[VMEM] + [HBM] * 5,
            out_shape=[one, act_s, act_s, act_s, table_s, table_s],
            scratch_shapes=[
                pltpu.VMEM((3, rows, width), bf16),
                pltpu.VMEM((rows, width), bf16),
                pltpu.VMEM((rows, width), jnp.float32),
                pltpu.VMEM((2, count, rows, 128), bf16),
                pltpu.VMEM((2, count, rows, 128), bf16),
                dma((2, count // UNROLL)),
                dma((2, count // UNROLL)),
                dma((5,)),
            ],
            input_output_aliases={7 + i: 1 + i for i in range(5)},
            compiler_params=params,
            cost_estimate=cost,
            name="forward",
        )(meta, up_rows, down_cols, far(tok), incoming, weights, far(after), *map(far, state))

    def backward(tick, incoming, saved, state):
        return pl.pallas_call(
            functools.partial(backward_kernel, tick, last),
            in_specs=[SMEM] * 3 + [HBM, VMEM, VMEM] + [HBM] * 7,
            out_specs=[VMEM] + [HBM] * 4,
            out_shape=[one, act_s, act_s, act_s, table_s],
            scratch_shapes=[
                pltpu.VMEM((3, rows, width), bf16),
                pltpu.VMEM((2, rows, width), bf16),
                pltpu.VMEM((rows, width), jnp.float32),
                pltpu.VMEM((2, count, rows, 128), bf16),
                pltpu.VMEM((2, count, rows, 128), bf16),
                dma((2, count // UNROLL)),
                dma((2, count // UNROLL)),
                dma((7,)),
            ],
            input_output_aliases={9 + i: 1 + i for i in range(4)},
            compiler_params=params,
            cost_estimate=cost,
            name="backward",
        )(meta, up_rows, down_cols, far(cotg), incoming, weights, *map(far, (*saved, *state)))

    blanks = blank_arrays(act, act, act, table, table, act, act, act, table)
    state, grad_state = blanks[:5], blanks[5:]
    incoming = grad_incoming = pltpu.with_memory_space_constraint(
        jnp.zeros((rows, width), bf16), pltpu.VMEM
    )
    for tick in range(groups + 2 * last):
        if tick < groups + last:
            result, *state = forward(tick, incoming, grad_state[0], state)
            live = [s for s in range(last) if 0 <= tick - s < groups]
            if live:
                incoming = relay(result, live, 1)
        back = tick - last
        if back >= 0:
            kin, kmid, _, slope, _ = state
            result, *grad_state = backward(back, grad_incoming, (kin, kmid, slope), grad_state)
            live = [s for s in range(1, sections) if 0 <= back - (last - s) < groups]
            if live:
                grad_incoming = relay(result, live, -1)
    kin, kmid, kout, slope, gated = state
    kdx, ktop, kinner, dpre = grad_state

    def flat(a):
        return a.reshape(tok_rows, width)

    gated = gated.reshape(2, count, tok_rows, 128)
    dpre = dpre.reshape(2, count, tok_rows, 128)
    totals = []
    for l, h, cot in ((1, kmid, ktop), (0, kin, kinner)):
        keep, send = block_grads(l, meta, up_rows, down_cols, flat(h), flat(cot), gated, dpre)
        total = add(keep, other_core(send))
        totals.append(total.reshape(count, SIDE, SIDE, 8, 128))
    chip = (place // (2 * SIDE), (place // 2) % SIDE)
    late, early = scatter_sum(*totals, chip)
    summed = jnp.stack([early, late])
    low, high = summed[:, :, :4], summed[:, :, 4:]
    mine = jnp.where(core == 0, low, high)
    theirs = other_core(jnp.where(core == 0, high, low))
    return (
        kout.reshape(1, tok_rows, width),
        kdx.reshape(1, tok_rows, width),
        jnp.where(core == 0, mine, theirs),
        jnp.where(core == 0, theirs, mine),
    )


def solution(mesh):
    in_specs = (
        P("dp", None),
        P("dp", None),
        P("section"),
        P("section", None),
        P("section", None),
        P("section", None, "dp", None),
        P("section", None, "dp", None),
    )
    out_specs = (
        P("section", "dp", None),
        P("section", "dp", None),
        P("section", None, "dp", None),
        P("section", None, "dp", None),
    )
    step = functools.partial(local, mesh.shape["section"])
    return jax.shard_map(step, mesh=mesh, in_specs=in_specs, out_specs=out_specs, check_vma=False)
```

```python
import functools

import jax
import jax.numpy as jnp
from jax import lax
from jax.experimental import pallas as pl
from jax.experimental.pallas import tpu as pltpu
from jax.sharding import PartitionSpec as P

GROUPS = 4
UNROLL = 28
EPS = 1e-05
SIDE = 4

root_coef = 0.7978845608028654
cubic_coef = 0.044715

HBM = pl.BlockSpec(memory_space=pltpu.HBM)
SMEM = pl.BlockSpec(memory_space=pltpu.SMEM)
VMEM = pl.BlockSpec(memory_space=pltpu.VMEM)
NN = (((1,), (0,)), ((), ()))
NT = (((1,), (1,)), ((), ()))
TN = (((0,), (0,)), ((), ()))


def dot(a, b, dims):
    return lax.dot_general(a, b, dims, preferred_element_type=jnp.float32)


def gelu_parts(p):
    square = p * p
    tangent = jnp.tanh(p * (root_coef + (root_coef * cubic_coef) * square))
    half = 0.5 * p
    gate = 0.5 + 0.5 * tangent
    slope = gate + half * (1.0 - tangent * tangent) * (
        root_coef + (3.0 * root_coef * cubic_coef) * square
    )
    return p * gate, slope


def lanes(block):
    return pl.ds(pl.multiple_of(block * 128, 128), 128)


def each_block(count, body, init, step=10):
    def run(i, carry):
        for u in range(step):
            carry = body(i * step + u, carry)
        return carry

    return lax.fori_loop(0, count // step, run, init)


def inverse_rms(h):
    rows, width = h.shape

    def add(k, totals):
        value = h[:, lanes(k)].astype(jnp.float32)
        return totals[1], totals[0] + value * value

    zero = jnp.zeros((rows, 128), jnp.float32)
    one, two = each_block(width // 128, add, (zero, zero))
    return lax.rsqrt(jnp.sum(one + two, axis=1, keepdims=True) * (1.0 / width) + EPS)


def table_copies(held, table, mb, sems):
    def copy(l, j, out=True):
        part = pl.ds(j * UNROLL, UNROLL)
        here, there = held.at[l, part], table.at[l, part, mb]
        if out:
            return pltpu.make_async_copy(here, there, sems.at[l, j])
        return pltpu.make_async_copy(there, here, sems.at[l, j])

    return copy


def run_pairs(count, before, body, after):
    def group(j, _):
        before(j)
        for u in range(0, UNROLL, 2):
            body(j * UNROLL + u)
        after(j)
        return 0

    lax.fori_loop(0, count // UNROLL, group, 0)


def pair_dot(left, right, weights, dims):
    rows = left.shape[0]
    both = jnp.concatenate([left, right], axis=0)
    axis = 1 if dims is NN else 0
    wide = dot(both, jnp.concatenate(weights, axis=axis), dims)
    return wide[:rows, :128], wide[rows:, 128:]


def forward_kernel(tick, meta, ups, downs, tok, inc, weights, after, *refs):
    (_, _, _, _, _, y, kin, kmid, kout, slope, gated,
     xv, normed, acc, sv, gv, ssem, gsem, iosem) = refs
    section = meta[0]
    mb = tick - section
    live = (mb >= 0) & (mb < GROUPS)
    layers = meta[1]
    two = layers > 1
    count, width = ups.shape[1], xv.shape[2]

    def io(n, src, dst):
        return pltpu.make_async_copy(src, dst, iosem.at[n])

    save_slope = table_copies(sv, slope, mb, ssem)
    save_gated = table_copies(gv, gated, mb, gsem)

    def saved(l):
        for j in range(count // UNROLL):
            save_slope(l, j).wait()
            save_gated(l, j).wait()

    def layer(l, _):
        x, out = xv.at[l], xv.at[l + 1]
        inv = inverse_rms(x)

        def start(k, _):
            value = x[:, lanes(k)].astype(jnp.float32)
            normed[:, lanes(k)] = (value * inv).astype(jnp.bfloat16)
            acc[:, lanes(k)] = value
            return 0

        each_block(width // 128, start, 0)
        up_at, down_at = 2 * l * count, (2 * l + 1) * count

        def body(f):
            pres = pair_dot(
                normed[:, lanes(ups[l, f])],
                normed[:, lanes(ups[l, f + 1])],
                (weights[up_at + f], weights[up_at + f + 1]),
                NN,
            )
            values = []
            for q, pre in enumerate(pres):
                value, grad = gelu_parts(pre)
                values.append(value.astype(jnp.bfloat16))
                gv[l, f + q] = values[q]
                sv[l, f + q] = grad.astype(jnp.bfloat16)
            mixed = pair_dot(
                *values, (weights[down_at + f], weights[down_at + f + 1]), NN
            )
            for q in range(2):
                at = lanes(downs[l, f + q])
                acc[:, at] = acc[:, at] + mixed[q]

        def after(j):
            save_slope(l, j).start()
            save_gated(l, j).start()

        run_pairs(count, lambda j: None, body, after)

        def finish(k, _):
            out[:, lanes(k)] = acc[:, lanes(k)].astype(jnp.bfloat16)
            return 0

        each_block(width // 128, finish, 0)
        return 0

    @pl.when(live)
    def _():
        @pl.when(section == 0)
        def _():
            io(0, tok.at[mb], xv.at[0]).start()

        @pl.when(section != 0)
        def _():
            io(0, inc, xv.at[0]).start()

        io(0, inc, xv.at[0]).wait()
        io(1, xv.at[0], kin.at[mb]).start()
        lax.fori_loop(0, layers, layer, 0)
        io(2, xv.at[layers], y).start()
        io(3, xv.at[layers], kout.at[mb]).start()

        @pl.when(two)
        def _():
            io(4, xv.at[1], kmid.at[mb]).start()
            io(4, xv.at[1], kmid.at[mb]).wait()
            saved(1)

        io(2, xv.at[layers], y).wait()
        io(3, xv.at[layers], kout.at[mb]).wait()
        io(1, xv.at[0], kin.at[mb]).wait()
        saved(0)


def backward_kernel(tick, last, meta, ups, downs, cotg, inc, weights, kin, kmid, slope, *refs):
    (_, _, _, _, dx, kdx, ktop, kinner, dpre,
     cv, hv, acc, sv, dv, ssem, dsem, iosem) = refs
    section = meta[0]
    mb = tick - (last - section)
    live = (mb >= 0) & (mb < GROUPS)
    layers = meta[1]
    two = layers > 1
    count, width = ups.shape[1], cv.shape[2]
    rows = cv.shape[1]

    def io(n, src, dst):
        return pltpu.make_async_copy(src, dst, iosem.at[n])

    slope_copy = table_copies(sv, slope, mb, ssem)
    save_dpre = table_copies(dv, dpre, mb, dsem)

    def load_slope(l):
        for j in range(count // UNROLL):
            slope_copy(l, j, False).start()

    def saved(l):
        for j in range(count // UNROLL):
            save_dpre(l, j).wait()

    def load_hidden(l, kept):
        return io(1 + l, kept.at[mb], hv.at[l])

    def layer(i, _):
        l = layers - 1 - i
        h, cot, out = hv.at[l], cv.at[l + 1], cv.at[l]
        load_hidden(l, kin).wait()
        inv = inverse_rms(h)

        def blank(k, _):
            acc[:, lanes(k)] = jnp.zeros((rows, 128), jnp.float32)
            return 0

        each_block(width // 128, blank, 0)
        up_at, down_at = 2 * l * count, (2 * l + 1) * count

        def body(f):
            inners = pair_dot(
                cot[:, lanes(downs[l, f])],
                cot[:, lanes(downs[l, f + 1])],
                (weights[down_at + f], weights[down_at + f + 1]),
                NT,
            )
            values = []
            for q, inner in enumerate(inners):
                scaled = inner * sv[l, f + q].astype(jnp.float32)
                values.append(scaled.astype(jnp.bfloat16))
                dv[l, f + q] = values[q]
            mixed = pair_dot(*values, (weights[up_at + f], weights[up_at + f + 1]), NT)
            for q in range(2):
                at = lanes(ups[l, f + q])
                acc[:, at] = acc[:, at] + mixed[q]

        run_pairs(
            count,
            lambda j: slope_copy(l, j, False).wait(),
            body,
            lambda j: save_dpre(l, j).start(),
        )

        def dots(k, totals):
            value = acc[:, lanes(k)] * h[:, lanes(k)].astype(jnp.float32)
            return totals[1], totals[0] + value

        zero = jnp.zeros((rows, 128), jnp.float32)
        one, other = each_block(width // 128, dots, (zero, zero))
        mean = jnp.sum(one + other, axis=1, keepdims=True) * inv * (1.0 / width)

        def finish(k, _):
            normal = h[:, lanes(k)].astype(jnp.float32) * inv
            value = cot[:, lanes(k)].astype(jnp.float32) + inv * (
                acc[:, lanes(k)] - normal * mean
            )
            out[:, lanes(k)] = value.astype(jnp.bfloat16)
            return 0

        each_block(width // 128, finish, 0)
        return 0

    @pl.when(live)
    def _():
        @pl.when(section == last)
        def _():
            io(0, cotg.at[mb], cv.at[layers]).start()

        @pl.when(section != last)
        def _():
            io(0, inc, cv.at[layers]).start()

        @pl.when(two)
        def _():
            load_hidden(1, kmid).start()
            load_slope(1)

        load_hidden(0, kin).start()
        load_slope(0)
        io(0, inc, cv.at[layers]).wait()
        lax.fori_loop(0, layers, layer, 0)
        io(5, cv.at[0], dx).start()
        io(6, cv.at[0], kdx.at[mb]).start()
        io(4, cv.at[1], kinner.at[mb]).start()

        @pl.when(two)
        def _():
            io(3, cv.at[2], ktop.at[mb]).start()
            io(3, cv.at[2], ktop.at[mb]).wait()
            saved(1)

        io(5, cv.at[0], dx).wait()
        io(6, cv.at[0], kdx.at[mb]).wait()
        io(4, cv.at[1], kinner.at[mb]).wait()
        saved(0)


def grad_kernel(l, meta, ups, downs, h, cot, gated, dpre, keep, send, normed):
    step = pl.program_id(0)
    count = keep.shape[2]
    width = h.shape[1]
    active = meta[1] > l

    @pl.when(active)
    def _():
        @pl.when(step == 0)
        def _():
            inv = inverse_rms(h)

            def start(k, _):
                normed[:, lanes(k)] = (h[:, lanes(k)].astype(jnp.float32) * inv).astype(
                    jnp.bfloat16
                )
                return 0

            each_block(width // 128, start, 0, 2)

        is_zero = meta[4] == 0
        for u in range(count):
            f = step * count + u
            up = dot(normed[:, lanes(ups[l, f])], dpre[0, u], TN)
            down = dot(gated[0, u], cot[:, lanes(downs[l, f])], TN)
            mine = jnp.where(is_zero, up, down).astype(jnp.bfloat16)
            other = jnp.where(is_zero, down, up).astype(jnp.bfloat16)
            for i in range(SIDE):
                for j in range(SIDE):
                    rows = slice((i * SIDE + j) * 8, (i * SIDE + j) * 8 + 8)
                    keep[i ^ meta[2], j ^ meta[3], u] = mine[rows]
                    send[i ^ meta[2], j ^ meta[3], u] = other[rows]

    @pl.when(jnp.logical_not(active))
    def _():
        keep[...] = jnp.zeros_like(keep)
        send[...] = jnp.zeros_like(send)


def block_grads(l, meta, ups, downs, h, cot, gated, dpre):
    count, width = ups.shape[1], h.shape[1]
    rows, per = h.shape[0], 14
    whole = pl.BlockSpec((rows, width), lambda i: (0, 0))
    table = pl.BlockSpec((1, per, rows, 128), lambda i: (l, i, 0, 0))
    out = pl.BlockSpec((SIDE, SIDE, per, 8, 128), lambda i: (0, 0, i, 0, 0))
    shape = jax.ShapeDtypeStruct((SIDE, SIDE, count, 8, 128), jnp.bfloat16)
    return pl.pallas_call(
        functools.partial(grad_kernel, l),
        grid=(count // per,),
        in_specs=[SMEM, SMEM, SMEM, whole, whole, table, table],
        out_specs=[out, out],
        out_shape=[shape, shape],
        scratch_shapes=[pltpu.VMEM((rows, width), jnp.bfloat16)],
        compiler_params=pltpu.CompilerParams(vmem_limit_bytes=56 << 20),
        name="grads",
    )(meta, ups, downs, h, cot, gated, dpre)


def swap(value, change):
    pairs = []
    for x in range(SIDE):
        for y in range(SIDE):
            for c in range(2):
                a, b, d = change(x, y, c)
                pairs.append(((x * SIDE + y) * 2 + c, (a * SIDE + b) * 2 + d))
    return lax.ppermute(value, "dp", pairs)


def along(axis, bits):
    if axis == 0:
        return lambda x, y, c: (x ^ bits, y, c)
    return lambda x, y, c: (x, y ^ bits, c)


def add(a, b):
    return (a.astype(jnp.float32) + b.astype(jnp.float32)).astype(jnp.bfloat16)


def other_core(value):
    return swap(value, lambda x, y, c: (x, y, 1 - c))


def parts(value, axis, picks):
    return jnp.concatenate(
        [lax.slice_in_dim(value, p, p + 1, axis=axis) for p in picks], axis=axis
    )


def scatter_sum(first, second):
    half = first.shape[2] // 2
    colors = [
        (first[:, :, :half], (1, 0), 1),
        (first[:, :, half:], (1, 0), 3),
        (second[:, :, :half], (0, 1), 1),
        (second[:, :, half:], (0, 1), 3),
    ]
    values = [c[0] for c in colors]
    for stage in range(4):
        fresh = []
        for value, (_, axes, bits) in zip(values, colors):
            axis = axes[stage // 2]
            if stage % 2 == 0:
                send = parts(value, axis, (bits, 2))
                keep = parts(value, axis, (0, bits ^ 2))
                got = swap(send, along(axis, bits))
            else:
                send = parts(value, axis, (1,))
                keep = parts(value, axis, (0,))
                got = swap(send, along(axis, bits ^ 2))
            fresh.append(add(keep, got))
        values = fresh
    shape = (2 * half,) + first.shape[3:]
    return (
        jnp.concatenate(values[:2], axis=2).reshape(shape),
        jnp.concatenate(values[2:], axis=2).reshape(shape),
    )


def gather_colors(up, down, core):
    mine = jnp.where(core == 0, up, down)
    got = other_core(jnp.where(core == 0, down, up))
    low, high = jnp.where(core == 0, mine, got), jnp.where(core == 0, got, mine)
    chip = jnp.concatenate([low, high], axis=2)
    half = chip.shape[1] // 2
    colors = [
        (chip[0, :half], (1, 0), 1),
        (chip[0, half:], (1, 0), 3),
        (chip[1, :half], (0, 1), 1),
        (chip[1, half:], (0, 1), 3),
    ]
    values = [c[0][None, None] for c in colors]
    for stage in range(4):
        fresh = []
        for value, (_, axes, bits) in zip(values, colors):
            axis = axes[stage // 2]
            if stage % 2 == 0:
                got = swap(value, along(axis, bits))
                fresh.append(jnp.concatenate([value, got], axis=axis))
                continue
            got = swap(value, along(axis, bits ^ 2))
            ones = [lax.slice_in_dim(v, p, p + 1, axis=axis) for v in (value, got) for p in (0, 1)]
            order = (0, 1, 3, 2) if bits == 1 else (0, 2, 3, 1)
            fresh.append(jnp.concatenate([ones[p] for p in order], axis=axis))
        values = fresh
    return values, [other_core(v) for v in values]


def place_kernel(meta, *refs):
    sources, out, held, sems = refs[:-3], refs[-3], refs[-2], refs[-1]
    total, half = len(sources), held.shape[3]

    def copy(n, source):
        return pltpu.make_async_copy(source, held.at[n], sems.at[n])

    for n, source in enumerate(sources):
        copy(n, source).start()

    def one(n, _):
        copy(n, sources[0]).wait()
        kind = (n & 1) ^ meta[4]
        base = (((n >> 2) * 2 + kind) * 2 + ((n >> 1) & 1)) * half

        def group(k, _):
            for u in range(4):
                f = k * 4 + u
                for i in range(SIDE):
                    for j in range(SIDE):
                        rows = slice((i * SIDE + j) * 8, (i * SIDE + j) * 8 + 8)
                        out[base + f, rows] = held[n, i ^ meta[2], j ^ meta[3], f]
            return 0

        lax.fori_loop(0, half // 4, group, 0)
        return 0

    lax.fori_loop(0, total, one, 0)


def place_blocks(meta, mine, theirs):
    sources = [v for pair in zip(mine, theirs) for v in pair]
    shape = sources[0].shape
    return pl.pallas_call(
        place_kernel,
        in_specs=[SMEM] + [HBM] * len(sources),
        out_specs=VMEM,
        out_shape=pltpu.VMEM((len(sources) * shape[2], 128, 128), jnp.bfloat16),
        scratch_shapes=[
            pltpu.VMEM((len(sources),) + shape, jnp.bfloat16),
            pltpu.SemaphoreType.DMA((len(sources),)),
        ],
        compiler_params=pltpu.CompilerParams(vmem_limit_bytes=20 << 20),
        name="place",
    )(meta, *map(far, sources))


def blank_arrays(*shapes):
    def kernel(*refs):
        pass

    return pl.pallas_call(
        kernel,
        out_shape=[pltpu.HBM(s, jnp.bfloat16) for s in shapes],
        out_specs=[HBM] * len(shapes),
        compiler_params=pltpu.CompilerParams(vmem_limit_bytes=1 << 20),
        name="blank",
    )()


def far(value):
    return pltpu.with_memory_space_constraint(value, pltpu.HBM)


def relay(value, live, steps):
    moved = lax.ppermute(value, "section", [(s, s + steps) for s in live])
    return pltpu.with_memory_space_constraint(moved, pltpu.VMEM)


def local(sections, tokens, cotangent, section_layers, up_rows, down_cols, up_blocks, down_blocks):
    last = sections - 1
    tok_rows, width = tokens.shape
    count = up_rows.shape[1]
    groups, rows = GROUPS, tok_rows // GROUPS
    place = lax.axis_index("dp").astype(jnp.int32)
    core = place % 2
    meta = jnp.stack(
        [
            lax.axis_index("section").astype(jnp.int32),
            section_layers[0],
            place // (2 * SIDE),
            (place // 2) % SIDE,
            core,
        ]
    )
    weights = place_blocks(meta, *gather_colors(up_blocks, down_blocks, core))
    tok = tokens.reshape(groups, rows, width)
    cotg = cotangent.reshape(groups, rows, width)
    act = (groups, rows, width)
    table = (2, count, groups, rows, 128)
    bf16 = jnp.bfloat16
    one = pltpu.VMEM((rows, width), bf16)
    act_s, table_s = pltpu.HBM(act, bf16), pltpu.HBM(table, bf16)
    dma = pltpu.SemaphoreType.DMA
    params = pltpu.CompilerParams(vmem_limit_bytes=20 << 20)
    flops = 8 * rows * count * 128 * 128
    cost = pl.CostEstimate(flops=flops, bytes_accessed=16 << 20, transcendentals=0)

    def forward(tick, incoming, after, state):
        return pl.pallas_call(
            functools.partial(forward_kernel, tick),
            in_specs=[SMEM] * 3 + [HBM, VMEM, VMEM] + [HBM] * 6,
            out_specs=[VMEM] + [HBM] * 5,
            out_shape=[one, act_s, act_s, act_s, table_s, table_s],
            scratch_shapes=[
                pltpu.VMEM((3, rows, width), bf16),
                pltpu.VMEM((rows, width), bf16),
                pltpu.VMEM((rows, width), jnp.float32),
                pltpu.VMEM((2, count, rows, 128), bf16),
                pltpu.VMEM((2, count, rows, 128), bf16),
                dma((2, count // UNROLL)),
                dma((2, count // UNROLL)),
                dma((5,)),
            ],
            input_output_aliases={7 + i: 1 + i for i in range(5)},
            compiler_params=params,
            cost_estimate=cost,
            name="forward",
        )(meta, up_rows, down_cols, far(tok), incoming, weights, far(after), *map(far, state))

    def backward(tick, incoming, saved, state):
        return pl.pallas_call(
            functools.partial(backward_kernel, tick, last),
            in_specs=[SMEM] * 3 + [HBM, VMEM, VMEM] + [HBM] * 7,
            out_specs=[VMEM] + [HBM] * 4,
            out_shape=[one, act_s, act_s, act_s, table_s],
            scratch_shapes=[
                pltpu.VMEM((3, rows, width), bf16),
                pltpu.VMEM((2, rows, width), bf16),
                pltpu.VMEM((rows, width), jnp.float32),
                pltpu.VMEM((2, count, rows, 128), bf16),
                pltpu.VMEM((2, count, rows, 128), bf16),
                dma((2, count // UNROLL)),
                dma((2, count // UNROLL)),
                dma((7,)),
            ],
            input_output_aliases={9 + i: 1 + i for i in range(4)},
            compiler_params=params,
            cost_estimate=cost,
            name="backward",
        )(meta, up_rows, down_cols, far(cotg), incoming, weights, *map(far, (*saved, *state)))

    blanks = blank_arrays(act, act, act, table, table, act, act, act, table)
    state, grad_state = blanks[:5], blanks[5:]
    incoming = grad_incoming = pltpu.with_memory_space_constraint(
        jnp.zeros((rows, width), bf16), pltpu.VMEM
    )
    for tick in range(groups + 2 * last):
        if tick < groups + last:
            result, *state = forward(tick, incoming, grad_state[0], state)
            live = [s for s in range(last) if 0 <= tick - s < groups]
            if live:
                incoming = relay(result, live, 1)
        back = tick - last
        if back >= 0:
            kin, kmid, _, slope, _ = state
            result, *grad_state = backward(back, grad_incoming, (kin, kmid, slope), grad_state)
            live = [s for s in range(1, sections) if 0 <= back - (last - s) < groups]
            if live:
                grad_incoming = relay(result, live, -1)
    kin, kmid, kout, slope, gated = state
    kdx, ktop, kinner, dpre = grad_state

    def flat(a):
        return a.reshape(tok_rows, width)

    gated = gated.reshape(2, count, tok_rows, 128)
    dpre = dpre.reshape(2, count, tok_rows, 128)
    totals = []
    for l, h, cot in ((1, kmid, ktop), (0, kin, kinner)):
        keep, send = block_grads(l, meta, up_rows, down_cols, flat(h), flat(cot), gated, dpre)
        totals.append(add(keep, other_core(send)))
    late, early = scatter_sum(*totals)
    summed = jnp.stack([early, late])
    low, high = summed[:, :, :4], summed[:, :, 4:]
    mine = jnp.where(core == 0, low, high)
    theirs = other_core(jnp.where(core == 0, high, low))
    return (
        kout.reshape(1, tok_rows, width),
        kdx.reshape(1, tok_rows, width),
        jnp.where(core == 0, mine, theirs),
        jnp.where(core == 0, theirs, mine),
    )


def solution(mesh):
    in_specs = (
        P("dp", None),
        P("dp", None),
        P("section"),
        P("section", None),
        P("section", None),
        P("section", None, "dp", None),
        P("section", None, "dp", None),
    )
    out_specs = (
        P("section", "dp", None),
        P("section", "dp", None),
        P("section", None, "dp", None),
        P("section", None, "dp", None),
    )
    step = functools.partial(local, mesh.shape["section"])
    return jax.shard_map(step, mesh=mesh, in_specs=in_specs, out_specs=out_specs, check_vma=False)
```

```python
import functools

import jax
import jax.numpy as jnp
from jax import lax
from jax.experimental import pallas as pl
from jax.experimental.pallas import tpu as pltpu
from jax.sharding import PartitionSpec as P

GROUPS = 4
UNROLL = 28
EPS = 1e-05
SIDE = 4

root_coef = 0.7978845608028654
cubic_coef = 0.044715

HBM = pl.BlockSpec(memory_space=pltpu.HBM)
SMEM = pl.BlockSpec(memory_space=pltpu.SMEM)
VMEM = pl.BlockSpec(memory_space=pltpu.VMEM)
NN = (((1,), (0,)), ((), ()))
NT = (((1,), (1,)), ((), ()))
TN = (((0,), (0,)), ((), ()))


def dot(a, b, dims):
    return lax.dot_general(a, b, dims, preferred_element_type=jnp.float32)


def gelu_parts(p):
    square = p * p
    tangent = jnp.tanh(p * (root_coef + (root_coef * cubic_coef) * square))
    half = 0.5 * p
    gate = 0.5 + 0.5 * tangent
    slope = gate + half * (1.0 - tangent * tangent) * (
        root_coef + (3.0 * root_coef * cubic_coef) * square
    )
    return p * gate, slope


def lanes(block):
    return pl.ds(pl.multiple_of(block * 128, 128), 128)


def each_block(count, body, init, step=10):
    def run(i, carry):
        for u in range(step):
            carry = body(i * step + u, carry)
        return carry

    return lax.fori_loop(0, count // step, run, init)


def inverse_rms(h):
    rows, width = h.shape

    def add(k, totals):
        value = h[:, lanes(k)].astype(jnp.float32)
        return totals[1], totals[0] + value * value

    zero = jnp.zeros((rows, 128), jnp.float32)
    one, two = each_block(width // 128, add, (zero, zero))
    return lax.rsqrt(jnp.sum(one + two, axis=1, keepdims=True) * (1.0 / width) + EPS)


def table_copies(held, table, mb, sems):
    def copy(l, j, out=True):
        part = pl.ds(j * UNROLL, UNROLL)
        here, there = held.at[l, part], table.at[l, part, mb]
        if out:
            return pltpu.make_async_copy(here, there, sems.at[l, j])
        return pltpu.make_async_copy(there, here, sems.at[l, j])

    return copy


def run_pairs(count, before, body, after):
    def group(j, _):
        before(j)
        for u in range(0, UNROLL, 2):
            body(j * UNROLL + u)
        after(j)
        return 0

    lax.fori_loop(0, count // UNROLL, group, 0)


def pair_dot(left, right, weights, dims):
    rows = left.shape[0]
    both = jnp.concatenate([left, right], axis=0)
    axis = 1 if dims is NN else 0
    wide = dot(both, jnp.concatenate(weights, axis=axis), dims)
    return wide[:rows, :128], wide[rows:, 128:]


def forward_kernel(tick, meta, ups, downs, tok, inc, weights, after, *refs):
    (_, _, _, _, _, y, kin, kmid, kout, slope, gated,
     xv, normed, acc, sv, gv, ssem, gsem, iosem) = refs
    section = meta[0]
    mb = tick - section
    live = (mb >= 0) & (mb < GROUPS)
    layers = meta[1]
    two = layers > 1
    count, width = ups.shape[1], xv.shape[2]

    def io(n, src, dst):
        return pltpu.make_async_copy(src, dst, iosem.at[n])

    save_slope = table_copies(sv, slope, mb, ssem)
    save_gated = table_copies(gv, gated, mb, gsem)

    def saved(l):
        for j in range(count // UNROLL):
            save_slope(l, j).wait()
            save_gated(l, j).wait()

    def layer(l, _):
        x, out = xv.at[l], xv.at[l + 1]
        inv = inverse_rms(x)

        def start(k, _):
            value = x[:, lanes(k)].astype(jnp.float32)
            normed[:, lanes(k)] = (value * inv).astype(jnp.bfloat16)
            acc[:, lanes(k)] = value
            return 0

        each_block(width // 128, start, 0)
        up_at, down_at = 2 * l * count, (2 * l + 1) * count

        def body(f):
            pres = pair_dot(
                normed[:, lanes(ups[l, f])],
                normed[:, lanes(ups[l, f + 1])],
                (weights[up_at + f], weights[up_at + f + 1]),
                NN,
            )
            values = []
            for q, pre in enumerate(pres):
                value, grad = gelu_parts(pre)
                values.append(value.astype(jnp.bfloat16))
                gv[l, f + q] = values[q]
                sv[l, f + q] = grad.astype(jnp.bfloat16)
            mixed = pair_dot(
                *values, (weights[down_at + f], weights[down_at + f + 1]), NN
            )
            for q in range(2):
                at = lanes(downs[l, f + q])
                acc[:, at] = acc[:, at] + mixed[q]

        def after(j):
            save_slope(l, j).start()
            save_gated(l, j).start()

        run_pairs(count, lambda j: None, body, after)

        def finish(k, _):
            out[:, lanes(k)] = acc[:, lanes(k)].astype(jnp.bfloat16)
            return 0

        each_block(width // 128, finish, 0)
        return 0

    @pl.when(live)
    def _():
        @pl.when(section == 0)
        def _():
            io(0, tok.at[mb], xv.at[0]).start()

        @pl.when(section != 0)
        def _():
            io(0, inc, xv.at[0]).start()

        io(0, inc, xv.at[0]).wait()
        io(1, xv.at[0], kin.at[mb]).start()
        lax.fori_loop(0, layers, layer, 0)
        io(2, xv.at[layers], y).start()
        io(3, xv.at[layers], kout.at[mb]).start()

        @pl.when(two)
        def _():
            io(4, xv.at[1], kmid.at[mb]).start()
            io(4, xv.at[1], kmid.at[mb]).wait()
            saved(1)

        io(2, xv.at[layers], y).wait()
        io(3, xv.at[layers], kout.at[mb]).wait()
        io(1, xv.at[0], kin.at[mb]).wait()
        saved(0)


def backward_kernel(tick, last, meta, ups, downs, cotg, inc, weights, kin, kmid, slope, *refs):
    (_, _, _, _, dx, kdx, ktop, kinner, dpre,
     cv, hv, acc, sv, dv, ssem, dsem, iosem) = refs
    section = meta[0]
    mb = tick - (last - section)
    live = (mb >= 0) & (mb < GROUPS)
    layers = meta[1]
    two = layers > 1
    count, width = ups.shape[1], cv.shape[2]
    rows = cv.shape[1]

    def io(n, src, dst):
        return pltpu.make_async_copy(src, dst, iosem.at[n])

    slope_copy = table_copies(sv, slope, mb, ssem)
    save_dpre = table_copies(dv, dpre, mb, dsem)

    def load_slope(l):
        for j in range(count // UNROLL):
            slope_copy(l, j, False).start()

    def saved(l):
        for j in range(count // UNROLL):
            save_dpre(l, j).wait()

    def load_hidden(l, kept):
        return io(1 + l, kept.at[mb], hv.at[l])

    def layer(i, _):
        l = layers - 1 - i
        h, cot, out = hv.at[l], cv.at[l + 1], cv.at[l]
        load_hidden(l, kin).wait()
        inv = inverse_rms(h)

        def blank(k, _):
            acc[:, lanes(k)] = jnp.zeros((rows, 128), jnp.float32)
            return 0

        each_block(width // 128, blank, 0)
        up_at, down_at = 2 * l * count, (2 * l + 1) * count

        def body(f):
            inners = pair_dot(
                cot[:, lanes(downs[l, f])],
                cot[:, lanes(downs[l, f + 1])],
                (weights[down_at + f], weights[down_at + f + 1]),
                NT,
            )
            values = []
            for q, inner in enumerate(inners):
                scaled = inner * sv[l, f + q].astype(jnp.float32)
                values.append(scaled.astype(jnp.bfloat16))
                dv[l, f + q] = values[q]
            mixed = pair_dot(*values, (weights[up_at + f], weights[up_at + f + 1]), NT)
            for q in range(2):
                at = lanes(ups[l, f + q])
                acc[:, at] = acc[:, at] + mixed[q]

        run_pairs(
            count,
            lambda j: slope_copy(l, j, False).wait(),
            body,
            lambda j: save_dpre(l, j).start(),
        )

        def dots(k, totals):
            value = acc[:, lanes(k)] * h[:, lanes(k)].astype(jnp.float32)
            return totals[1], totals[0] + value

        zero = jnp.zeros((rows, 128), jnp.float32)
        one, other = each_block(width // 128, dots, (zero, zero))
        mean = jnp.sum(one + other, axis=1, keepdims=True) * inv * (1.0 / width)

        def finish(k, _):
            normal = h[:, lanes(k)].astype(jnp.float32) * inv
            value = cot[:, lanes(k)].astype(jnp.float32) + inv * (
                acc[:, lanes(k)] - normal * mean
            )
            out[:, lanes(k)] = value.astype(jnp.bfloat16)
            return 0

        each_block(width // 128, finish, 0)
        return 0

    @pl.when(live)
    def _():
        @pl.when(section == last)
        def _():
            io(0, cotg.at[mb], cv.at[layers]).start()

        @pl.when(section != last)
        def _():
            io(0, inc, cv.at[layers]).start()

        @pl.when(two)
        def _():
            load_hidden(1, kmid).start()
            load_slope(1)

        load_hidden(0, kin).start()
        load_slope(0)
        io(0, inc, cv.at[layers]).wait()
        lax.fori_loop(0, layers, layer, 0)
        io(5, cv.at[0], dx).start()
        io(6, cv.at[0], kdx.at[mb]).start()
        io(4, cv.at[1], kinner.at[mb]).start()

        @pl.when(two)
        def _():
            io(3, cv.at[2], ktop.at[mb]).start()
            io(3, cv.at[2], ktop.at[mb]).wait()
            saved(1)

        io(5, cv.at[0], dx).wait()
        io(6, cv.at[0], kdx.at[mb]).wait()
        io(4, cv.at[1], kinner.at[mb]).wait()
        saved(0)


def grad_kernel(l, meta, ups, downs, h, cot, gated, dpre, keep, send, normed):
    step = pl.program_id(0)
    count = keep.shape[2]
    width = h.shape[1]
    active = meta[1] > l

    @pl.when(active)
    def _():
        @pl.when(step == 0)
        def _():
            inv = inverse_rms(h)

            def start(k, _):
                normed[:, lanes(k)] = (h[:, lanes(k)].astype(jnp.float32) * inv).astype(
                    jnp.bfloat16
                )
                return 0

            each_block(width // 128, start, 0, 2)

        is_zero = meta[4] == 0
        for u in range(count):
            f = step * count + u
            up = dot(normed[:, lanes(ups[l, f])], dpre[0, u], TN)
            down = dot(gated[0, u], cot[:, lanes(downs[l, f])], TN)
            mine = jnp.where(is_zero, up, down).astype(jnp.bfloat16)
            other = jnp.where(is_zero, down, up).astype(jnp.bfloat16)
            for i in range(SIDE):
                for j in range(SIDE):
                    rows = slice((i * SIDE + j) * 8, (i * SIDE + j) * 8 + 8)
                    keep[i ^ meta[2], j ^ meta[3], u] = mine[rows]
                    send[i ^ meta[2], j ^ meta[3], u] = other[rows]

    @pl.when(jnp.logical_not(active))
    def _():
        keep[...] = jnp.zeros_like(keep)
        send[...] = jnp.zeros_like(send)


def block_grads(l, meta, ups, downs, h, cot, gated, dpre):
    count, width = ups.shape[1], h.shape[1]
    rows, per = h.shape[0], 14
    whole = pl.BlockSpec((rows, width), lambda i: (0, 0))
    table = pl.BlockSpec((1, per, rows, 128), lambda i: (l, i, 0, 0))
    out = pl.BlockSpec((SIDE, SIDE, per, 8, 128), lambda i: (0, 0, i, 0, 0))
    shape = jax.ShapeDtypeStruct((SIDE, SIDE, count, 8, 128), jnp.bfloat16)
    return pl.pallas_call(
        functools.partial(grad_kernel, l),
        grid=(count // per,),
        in_specs=[SMEM, SMEM, SMEM, whole, whole, table, table],
        out_specs=[out, out],
        out_shape=[shape, shape],
        scratch_shapes=[pltpu.VMEM((rows, width), jnp.bfloat16)],
        compiler_params=pltpu.CompilerParams(vmem_limit_bytes=56 << 20),
        name="grads",
    )(meta, ups, downs, h, cot, gated, dpre)


def swap(value, change):
    pairs = []
    for x in range(SIDE):
        for y in range(SIDE):
            for c in range(2):
                a, b, d = change(x, y, c)
                pairs.append(((x * SIDE + y) * 2 + c, (a * SIDE + b) * 2 + d))
    return lax.ppermute(value, "dp", pairs)


def along(axis, bits):
    if axis == 0:
        return lambda x, y, c: (x ^ bits, y, c)
    return lambda x, y, c: (x, y ^ bits, c)


def add(a, b):
    return (a.astype(jnp.float32) + b.astype(jnp.float32)).astype(jnp.bfloat16)


def other_core(value):
    return swap(value, lambda x, y, c: (x, y, 1 - c))


def parts(value, axis, picks):
    return jnp.concatenate(
        [lax.slice_in_dim(value, p, p + 1, axis=axis) for p in picks], axis=axis
    )


def scatter_sum(first, second):
    half = first.shape[2] // 2
    colors = [
        (first[:, :, :half], (1, 0), 1),
        (first[:, :, half:], (1, 0), 3),
        (second[:, :, :half], (0, 1), 1),
        (second[:, :, half:], (0, 1), 3),
    ]
    values = [c[0] for c in colors]
    for stage in range(4):
        fresh = []
        for value, (_, axes, bits) in zip(values, colors):
            axis = axes[stage // 2]
            if stage % 2 == 0:
                send = parts(value, axis, (bits, 2))
                keep = parts(value, axis, (0, bits ^ 2))
                got = swap(send, along(axis, bits))
            else:
                send = parts(value, axis, (1,))
                keep = parts(value, axis, (0,))
                got = swap(send, along(axis, bits ^ 2))
            fresh.append(add(keep, got))
        values = lax.optimization_barrier(fresh)
    shape = (2 * half,) + first.shape[3:]
    return (
        jnp.concatenate(values[:2], axis=2).reshape(shape),
        jnp.concatenate(values[2:], axis=2).reshape(shape),
    )


def gather_colors(up, down, core):
    mine = jnp.where(core == 0, up, down)
    got = other_core(jnp.where(core == 0, down, up))
    low, high = jnp.where(core == 0, mine, got), jnp.where(core == 0, got, mine)
    chip = jnp.concatenate([low, high], axis=2)
    half = chip.shape[1] // 2
    colors = [
        (chip[0, :half], (1, 0), 1),
        (chip[0, half:], (1, 0), 3),
        (chip[1, :half], (0, 1), 1),
        (chip[1, half:], (0, 1), 3),
    ]
    values = lax.optimization_barrier([c[0][None, None] for c in colors])
    for stage in range(4):
        fresh = []
        for value, (_, axes, bits) in zip(values, colors):
            axis = axes[stage // 2]
            if stage % 2 == 0:
                got = swap(value, along(axis, bits))
                fresh.append(jnp.concatenate([value, got], axis=axis))
                continue
            got = swap(value, along(axis, bits ^ 2))
            ones = [lax.slice_in_dim(v, p, p + 1, axis=axis) for v in (value, got) for p in (0, 1)]
            order = (0, 1, 3, 2) if bits == 1 else (0, 2, 3, 1)
            fresh.append(jnp.concatenate([ones[p] for p in order], axis=axis))
        values = lax.optimization_barrier(fresh)
    return values, [other_core(v) for v in values]


def place_kernel(meta, *refs):
    sources, out, held, sems = refs[:-3], refs[-3], refs[-2], refs[-1]
    total, half = len(sources), held.shape[3]

    def copy(n, source):
        return pltpu.make_async_copy(source, held.at[n], sems.at[n])

    for n, source in enumerate(sources):
        copy(n, source).start()

    def one(n, _):
        copy(n, sources[0]).wait()
        kind = (n & 1) ^ meta[4]
        base = (((n >> 2) * 2 + kind) * 2 + ((n >> 1) & 1)) * half

        def group(k, _):
            for u in range(4):
                f = k * 4 + u
                for i in range(SIDE):
                    for j in range(SIDE):
                        rows = slice((i * SIDE + j) * 8, (i * SIDE + j) * 8 + 8)
                        out[base + f, rows] = held[n, i ^ meta[2], j ^ meta[3], f]
            return 0

        lax.fori_loop(0, half // 4, group, 0)
        return 0

    lax.fori_loop(0, total, one, 0)


def place_blocks(meta, mine, theirs):
    sources = [v for pair in zip(mine, theirs) for v in pair]
    shape = sources[0].shape
    return pl.pallas_call(
        place_kernel,
        in_specs=[SMEM] + [HBM] * len(sources),
        out_specs=VMEM,
        out_shape=pltpu.VMEM((len(sources) * shape[2], 128, 128), jnp.bfloat16),
        scratch_shapes=[
            pltpu.VMEM((len(sources),) + shape, jnp.bfloat16),
            pltpu.SemaphoreType.DMA((len(sources),)),
        ],
        compiler_params=pltpu.CompilerParams(vmem_limit_bytes=20 << 20),
        name="place",
    )(meta, *map(far, sources))


def blank_arrays(*shapes):
    def kernel(*refs):
        pass

    return pl.pallas_call(
        kernel,
        out_shape=[pltpu.HBM(s, jnp.bfloat16) for s in shapes],
        out_specs=[HBM] * len(shapes),
        compiler_params=pltpu.CompilerParams(vmem_limit_bytes=1 << 20),
        name="blank",
    )()


def far(value):
    return pltpu.with_memory_space_constraint(value, pltpu.HBM)


def relay(value, live, steps):
    moved = lax.ppermute(value, "section", [(s, s + steps) for s in live])
    return pltpu.with_memory_space_constraint(moved, pltpu.VMEM)


def local(sections, tokens, cotangent, section_layers, up_rows, down_cols, up_blocks, down_blocks):
    last = sections - 1
    tok_rows, width = tokens.shape
    count = up_rows.shape[1]
    groups, rows = GROUPS, tok_rows // GROUPS
    place = lax.axis_index("dp").astype(jnp.int32)
    core = place % 2
    meta = jnp.stack(
        [
            lax.axis_index("section").astype(jnp.int32),
            section_layers[0],
            place // (2 * SIDE),
            (place // 2) % SIDE,
            core,
        ]
    )
    weights = place_blocks(meta, *gather_colors(up_blocks, down_blocks, core))
    tok = tokens.reshape(groups, rows, width)
    cotg = cotangent.reshape(groups, rows, width)
    act = (groups, rows, width)
    table = (2, count, groups, rows, 128)
    bf16 = jnp.bfloat16
    one = pltpu.VMEM((rows, width), bf16)
    act_s, table_s = pltpu.HBM(act, bf16), pltpu.HBM(table, bf16)
    dma = pltpu.SemaphoreType.DMA
    params = pltpu.CompilerParams(vmem_limit_bytes=20 << 20)
    flops = 8 * rows * count * 128 * 128
    cost = pl.CostEstimate(flops=flops, bytes_accessed=16 << 20, transcendentals=0)

    def forward(tick, incoming, after, state):
        return pl.pallas_call(
            functools.partial(forward_kernel, tick),
            in_specs=[SMEM] * 3 + [HBM, VMEM, VMEM] + [HBM] * 6,
            out_specs=[VMEM] + [HBM] * 5,
            out_shape=[one, act_s, act_s, act_s, table_s, table_s],
            scratch_shapes=[
                pltpu.VMEM((3, rows, width), bf16),
                pltpu.VMEM((rows, width), bf16),
                pltpu.VMEM((rows, width), jnp.float32),
                pltpu.VMEM((2, count, rows, 128), bf16),
                pltpu.VMEM((2, count, rows, 128), bf16),
                dma((2, count // UNROLL)),
                dma((2, count // UNROLL)),
                dma((5,)),
            ],
            input_output_aliases={7 + i: 1 + i for i in range(5)},
            compiler_params=params,
            cost_estimate=cost,
            name="forward",
        )(meta, up_rows, down_cols, far(tok), incoming, weights, far(after), *map(far, state))

    def backward(tick, incoming, saved, state):
        return pl.pallas_call(
            functools.partial(backward_kernel, tick, last),
            in_specs=[SMEM] * 3 + [HBM, VMEM, VMEM] + [HBM] * 7,
            out_specs=[VMEM] + [HBM] * 4,
            out_shape=[one, act_s, act_s, act_s, table_s],
            scratch_shapes=[
                pltpu.VMEM((3, rows, width), bf16),
                pltpu.VMEM((2, rows, width), bf16),
                pltpu.VMEM((rows, width), jnp.float32),
                pltpu.VMEM((2, count, rows, 128), bf16),
                pltpu.VMEM((2, count, rows, 128), bf16),
                dma((2, count // UNROLL)),
                dma((2, count // UNROLL)),
                dma((7,)),
            ],
            input_output_aliases={9 + i: 1 + i for i in range(4)},
            compiler_params=params,
            cost_estimate=cost,
            name="backward",
        )(meta, up_rows, down_cols, far(cotg), incoming, weights, *map(far, (*saved, *state)))

    blanks = blank_arrays(act, act, act, table, table, act, act, act, table)
    state, grad_state = blanks[:5], blanks[5:]
    incoming = grad_incoming = pltpu.with_memory_space_constraint(
        jnp.zeros((rows, width), bf16), pltpu.VMEM
    )
    for tick in range(groups + 2 * last):
        if tick < groups + last:
            result, *state = forward(tick, incoming, grad_state[0], state)
            live = [s for s in range(last) if 0 <= tick - s < groups]
            if live:
                incoming = relay(result, live, 1)
        back = tick - last
        if back >= 0:
            kin, kmid, _, slope, _ = state
            result, *grad_state = backward(back, grad_incoming, (kin, kmid, slope), grad_state)
            live = [s for s in range(1, sections) if 0 <= back - (last - s) < groups]
            if live:
                grad_incoming = relay(result, live, -1)
    kin, kmid, kout, slope, gated = state
    kdx, ktop, kinner, dpre = grad_state

    def flat(a):
        return a.reshape(tok_rows, width)

    gated = gated.reshape(2, count, tok_rows, 128)
    dpre = dpre.reshape(2, count, tok_rows, 128)
    totals = []
    for l, h, cot in ((1, kmid, ktop), (0, kin, kinner)):
        keep, send = block_grads(l, meta, up_rows, down_cols, flat(h), flat(cot), gated, dpre)
        totals.append(add(keep, other_core(send)))
    late, early = scatter_sum(*totals)
    summed = jnp.stack([early, late])
    low, high = summed[:, :, :4], summed[:, :, 4:]
    mine = jnp.where(core == 0, low, high)
    theirs = other_core(jnp.where(core == 0, high, low))
    return (
        kout.reshape(1, tok_rows, width),
        kdx.reshape(1, tok_rows, width),
        jnp.where(core == 0, mine, theirs),
        jnp.where(core == 0, theirs, mine),
    )


def solution(mesh):
    in_specs = (
        P("dp", None),
        P("dp", None),
        P("section"),
        P("section", None),
        P("section", None),
        P("section", None, "dp", None),
        P("section", None, "dp", None),
    )
    out_specs = (
        P("section", "dp", None),
        P("section", "dp", None),
        P("section", None, "dp", None),
        P("section", None, "dp", None),
    )
    step = functools.partial(local, mesh.shape["section"])
    return jax.shard_map(step, mesh=mesh, in_specs=in_specs, out_specs=out_specs, check_vma=False)
```
